32 devices in a mesh: freq: 2 (over y), slab: 16 (over z, x, core).
Axes of the slice: x: 2, y: 2, z: 4, core: 2. Of those that a mesh axis runs over, the one named last changes fastest.
Arguments:
- wavefield: float32 [2, 2, 2048, 2048], P(None, 'freq', 'slab'), may hold values from -6 to 6
- freqs: float32 [2], P('freq'), may hold values from 0.15 to 0.45
- velocity: float32 [3, 2048, 2048], P(None, 'slab', 'freq'), may hold values from 0.7 to 1.6
- ref_slow: float32 [3, 2], replicated, may hold values from 0.6 to 1.5, as said below
Outputs:
- migrated: float32 [2, 2, 2048, 2048], P(None, 'freq', 'slab')
The draws below stay inside these ranges and needn't reach their ends.
Inputs may be any that keep to these rules, and one draw needn't show every extreme that they name: ref_slow[d, 1] - ref_slow[d, 0] lies between 0.3 and 0.6 for every depth step.
All inputs are finite; a program needn't handle non-finite values.
Results may differ from the reference program's by a relative error of at most 0.0003.
Values sent between devices are 32-bit elements; how exact they have to be, the bound alone decides.
A program may use at most 64 MiB of HBM per device.

```python
import math
import jax
import jax.numpy as jnp
from jax import lax

NX = 2048
NY = 2048
DEPTH = 3
FREQ = 2


def draw_ref_slow(key, part):
    first_key, second_key = jax.random.split(jax.random.fold_in(key, 11))
    lower = jax.random.uniform(first_key, (DEPTH,), jnp.float32, 0.6, 0.9)
    spacing = jax.random.uniform(second_key, (DEPTH,), jnp.float32, 0.3, 0.6)
    return jnp.stack([lower, lower + spacing], axis=1)


def block_levels(rng, extent, cuts, smallest, largest):
    def one(dim, parts):
        steps = jax.random.uniform(jax.random.fold_in(jax.random.fold_in(rng, 6), dim), (parts,), jnp.float32, smallest / len(cuts), largest / len(cuts))
        return jnp.repeat(jnp.exp(steps), extent[dim] // parts).reshape((-1,) + (1,) * (len(extent) - dim - 1))

    loudness = one(*cuts[0])
    for cut in cuts[1:]:
        loudness = loudness * one(*cut)
    return loudness


def bell_draw(rng, extent, deviation, bound, cuts=(), kind=jnp.bfloat16):
    factor_of = block_levels(rng, extent, cuts, -0.22, 0.18) if cuts else 1.0
    values = jax.random.normal(rng, extent, jnp.float32) * deviation * factor_of
    return jnp.minimum(jnp.maximum(values, -bound), bound).astype(kind)


def setup_inputs(seed: int = 0) -> dict:
    splits = jax.random.split(jax.random.key(seed), 5)
    return {
        "wavefield": bell_draw(splits[0], (2, FREQ, NX, NY), 1.0, 6.0, ((1, 2), (2, 16)), jnp.float32),
        "freqs": jnp.clip(0.15 + 0.29999998 * jax.random.uniform(splits[1], (FREQ,), jnp.float32) ** block_levels(splits[1], (FREQ,), ((0, 2),), -0.2, 0.2), 0.15, 0.45),
        "velocity": jnp.clip(0.7 + 0.90000004 * jax.random.uniform(splits[2], (DEPTH, NX, NY), jnp.float32) ** block_levels(splits[2], (DEPTH, NX, NY), ((1, 16), (2, 2)), -0.2, 0.2), 0.7, 1.6),
        "ref_slow": draw_ref_slow(jax.random.fold_in(splits[4], 71), 0),
    }


def centred(length):
    index = jnp.arange(length, dtype=jnp.float32)
    return jnp.where(index < length // 2, index, index - length) / length

def reference(wavefield, freqs, velocity, ref_slow):
    depth_step = 2.0
    two_pi = 2.0 * math.pi
    field = lax.complex(wavefield[0], wavefield[1])
    along_x = centred(NX)
    along_y = centred(NY)
    square = along_x[:, None] ** 2 + along_y[None, :] ** 2
    freq_col = freqs[:, None, None]
    for level in range(DEPTH):
        spectrum = jnp.fft.fft2(field, norm='ortho')
        slowness = 1.0 / velocity[level]
        lower = ref_slow[level, 0]
        upper = ref_slow[level, 1]
        upper_weight = jnp.clip((slowness - lower) / (upper - lower), 0.0, 1.0)
        weights = [1.0 - upper_weight, upper_weight]
        total = jnp.zeros_like(field)
        for branch in range(2):
            slow_ref = ref_slow[level, branch]
            target = (freq_col * slow_ref) ** 2 - square[None]
            angle = two_pi * depth_step * jnp.sqrt(jnp.abs(target))
            live = target >= 0
            shift = lax.complex(jnp.where(live, jnp.cos(angle), jnp.exp(-angle)), jnp.where(live, jnp.sin(angle), jnp.zeros_like(angle)))
            moved = jnp.fft.ifft2(spectrum * shift, norm='ortho')
            theta = two_pi * depth_step * freq_col * (slowness - slow_ref)[None]
            weight = weights[branch][None]
            total = total + weight * lax.complex(jnp.cos(theta), jnp.sin(theta)) * moved
        field = total
    return jnp.stack([jnp.real(field), jnp.imag(field)])
```

```python
import functools
import math

import jax
import jax.numpy as jnp
import numpy as np
from jax import lax
from jax.experimental import pallas as pl
from jax.experimental.pallas import tpu as pltpu
from jax.sharding import PartitionSpec as P

two_pi = 2.0 * math.pi
depth_step = 2.0


def dft_matrix(length, sign):
    index = jnp.arange(length, dtype=jnp.int32)
    product = index[:, None] * index[None, :] % length
    angle = sign * two_pi / length * product.astype(jnp.float32)
    scale = 1.0 / math.sqrt(length)
    return (jnp.cos(angle) * scale, jnp.sin(angle) * scale)


def twiddle(outer, inner, sign):
    length = outer * inner
    product = (
        jnp.arange(outer, dtype=jnp.int32)[:, None]
        * jnp.arange(inner, dtype=jnp.int32)[None, :]
        % length
    )
    angle = sign * two_pi / length * product.astype(jnp.float32)
    return (jnp.cos(angle), jnp.sin(angle))


def complex_mix(form, mat_real, mat_imag, data_real, data_imag):

    def product(matrix, data):
        return jnp.einsum(form, matrix, data, precision=lax.Precision.HIGHEST)

    return (
        product(mat_real, data_real) - product(mat_imag, data_imag),
        product(mat_real, data_imag) + product(mat_imag, data_real),
    )


def transform(real, imag, trailing, sign):
    length = real.shape[-2] if trailing else real.shape[-1]
    inner = min(length, 128)
    outer = length // inner
    outer_real, outer_imag = dft_matrix(outer, sign)
    inner_real, inner_imag = dft_matrix(inner, sign)
    turn_real, turn_imag = twiddle(outer, inner, sign)
    if trailing:
        leading = real.shape[:-2]
        tail = real.shape[-1:]
        form_outer = "ka,...abm->...kbm"
        form_inner = "bj,...kbm->...kjm"
        turn_real = turn_real[:, :, None]
        turn_imag = turn_imag[:, :, None]
    else:
        leading = real.shape[:-1]
        tail = ()
        form_outer = "ka,...ab->...kb"
        form_inner = "bj,...kb->...kj"
    split_shape = leading + (outer, inner) + tail
    real = real.reshape(split_shape)
    imag = imag.reshape(split_shape)
    if sign < 0:
        real, imag = complex_mix(form_outer, outer_real, outer_imag, real, imag)
        real, imag = (real * turn_real - imag * turn_imag, real * turn_imag + imag * turn_real)
        real, imag = complex_mix(form_inner, inner_real, inner_imag, real, imag)
    else:
        real, imag = complex_mix(form_inner, inner_real, inner_imag, real, imag)
        real, imag = (real * turn_real - imag * turn_imag, real * turn_imag + imag * turn_real)
        real, imag = complex_mix(form_outer, outer_real, outer_imag, real, imag)
    joined = leading + (length,) + tail
    return (real.reshape(joined), imag.reshape(joined))


def wave_numbers(positions, length):
    inner = min(length, 128)
    outer = length // inner
    number = positions // inner + outer * (positions % inner)
    number = jnp.where(number < length // 2, number, number - length)
    return number.astype(jnp.float32) / length


def forward_x(items):
    real, imag = transform(items[0], items[1], True, -1)
    return jnp.stack((real, imag))


def inverse_y(items):
    real, imag = transform(items[:, 0], items[:, 1], False, 1)
    return jnp.stack((real, imag), axis=1)


def shards_generic(wavefield, freqs, velocity, ref_slow):
    slabs = lax.axis_size("slab")
    slab_index = lax.axis_index("slab")
    rows = wavefield.shape[2]
    width_x = rows * slabs
    width_y = wavefield.shape[3]
    columns = width_y // slabs
    depth = ref_slow.shape[0]
    along_x = wave_numbers(jnp.arange(width_x, dtype=jnp.int32), width_x)
    along_y = wave_numbers(slab_index * columns + jnp.arange(columns, dtype=jnp.int32), width_y)
    square = along_x[:, None] ** 2 + along_y[None, :] ** 2
    freq_col = freqs[:, None, None]

    def advance(level, field):
        local_tile = lax.dynamic_index_in_dim(velocity, level, 0, keepdims=False)
        tile = lax.all_gather(local_tile, "freq", axis=1, tiled=True)
        real, imag = transform(field[0], field[1], False, -1)
        spectrum = forward_x(
            lax.all_to_all(jnp.stack((real, imag)), "slab", split_axis=3, concat_axis=2, tiled=True)
        )
        slow_pair = lax.dynamic_index_in_dim(ref_slow, level, 0, keepdims=False)
        slowness = 1.0 / tile
        upper_weight = jnp.clip((slowness - slow_pair[0]) / (slow_pair[1] - slow_pair[0]), 0.0, 1.0)
        weights = [1.0 - upper_weight, upper_weight]
        shifted = []
        for branch in range(2):
            target = (freq_col * slow_pair[branch]) ** 2 - square[None]
            angle = two_pi * depth_step * jnp.sqrt(jnp.abs(target))
            live = target >= 0
            prop_real = jnp.where(live, jnp.cos(angle), jnp.exp(-angle))
            prop_imag = jnp.where(live, jnp.sin(angle), jnp.zeros_like(angle))
            spec_real = spectrum[0] * prop_real - spectrum[1] * prop_imag
            spec_imag = spectrum[0] * prop_imag + spectrum[1] * prop_real
            back_real, back_imag = transform(spec_real, spec_imag, True, 1)
            shifted.append(jnp.stack((back_real, back_imag)))
        pieces = []
        for branch in range(2):
            moved = lax.all_to_all(shifted[branch], "slab", split_axis=2, concat_axis=3, tiled=True)
            pieces.append(inverse_y(moved[None])[0])
        spatial = jnp.stack(pieces)
        new_real = jnp.zeros_like(field[0])
        new_imag = jnp.zeros_like(field[1])
        for branch in range(2):
            theta = two_pi * depth_step * freq_col * (slowness - slow_pair[branch])[None]
            weight = weights[branch][None]
            cosine = jnp.cos(theta)
            sine = jnp.sin(theta)
            part_real = spatial[branch, 0]
            part_imag = spatial[branch, 1]
            new_real = new_real + weight * (cosine * part_real - sine * part_imag)
            new_imag = new_imag + weight * (cosine * part_imag + sine * part_real)
        return jnp.stack((new_real, new_imag))

    return lax.fori_loop(0, depth, advance, wavefield)


LANES = 128
ROWS = 8
VMEM_LIMIT = 56 * 2**20


def turn(numerator, denominator, sign):
    angle = sign * 2.0 * np.pi * ((numerator % denominator) / denominator)
    return (np.cos(angle), np.sin(angle))


def times(real, imag, c, s):
    if abs(s) < 1e-12:
        return (real, imag) if c > 0 else (-real, -imag)
    if abs(c) < 1e-12:
        return (-imag, real) if s > 0 else (imag, -real)
    if abs(abs(c) - abs(s)) < 1e-12:
        k = float(abs(c))
        a, b = (k if c > 0 else -k), (s > 0) == (c > 0)
        if b:
            return ((real - imag) * a, (real + imag) * a)
        return ((real + imag) * a, (imag - real) * a)
    c, s = float(c), float(s)
    return (real * c - imag * s, real * s + imag * c)


def small_fft(real, imag, sign):
    count = len(real)
    if count == 1:
        return real, imag
    er, ei = small_fft(real[0::2], imag[0::2], sign)
    odd_r, odd_i = small_fft(real[1::2], imag[1::2], sign)
    low, high = [], []
    for k in range(count // 2):
        tr, ti = times(odd_r[k], odd_i[k], *turn(k, count, sign))
        low.append((er[k] + tr, ei[k] + ti))
        high.append((er[k] - tr, ei[k] - ti))
    both = low + high
    return [v[0] for v in both], [v[1] for v in both]


def halves(x):
    high = x.astype(jnp.bfloat16)
    low = (x - high.astype(jnp.float32)).astype(jnp.bfloat16)
    return high, low


def product(a, b):
    def dot(p, q):
        return jnp.dot(p, q, preferred_element_type=jnp.float32)

    return dot(a[0], b[0]) + (dot(a[0], b[1]) + dot(a[1], b[0]))


def matrix_of(inner, length, sign, left):
    index = np.arange(inner)
    angle = sign * 2.0 * np.pi * ((index[:, None] * index[None, :]) % inner) / inner
    c = np.cos(angle) / np.sqrt(length)
    s = np.sin(angle) / np.sqrt(length)
    full = np.block([[c, -s], [s, c]]) if left else np.block([[c, s], [-s, c]])
    full = full.astype(np.float32)
    high = full.astype(jnp.bfloat16)
    low = (full - high.astype(np.float32)).astype(jnp.bfloat16)
    return np.stack([high, low])


def twiddle_table(outer, inner, rows):
    c, s = turn(np.arange(outer)[:, None] * np.arange(inner)[None, :], outer * inner, -1)
    both = np.stack([c, s], axis=1).astype(np.float32)
    if rows:
        return np.ascontiguousarray(np.broadcast_to(both[:, :, :, None], (outer, 2, inner, LANES)))
    return np.ascontiguousarray(np.broadcast_to(both[:, :, None, :], (outer, 2, ROWS, inner)))


def cosine_terms():
    z = 0.125 + 0.125 * np.cos(np.pi * (np.arange(400) + 0.5) / 400)
    r = np.sqrt(z)

    def fit(values, degree):
        poly = np.polynomial.Chebyshev.fit(z, values, degree, domain=[0.0, 0.25])
        poly = poly.convert(kind=np.polynomial.Polynomial)
        return [float(np.float32(v)) for v in poly.coef]

    return fit(np.cos(2 * np.pi * r), 8), fit(np.sin(2 * np.pi * r) / r, 7)


COS_TERMS, SIN_TERMS = cosine_terms()


def horner(terms, z):
    value = z * terms[-1] + terms[-2]
    for term in terms[-3::-1]:
        value = value * z + term
    return value


def circle(turns):
    rest = turns - jnp.round(turns)
    z = rest * rest
    return horner(COS_TERMS, z), rest * horner(SIN_TERMS, z)


def spread_kernel(outer, length, scal, fy2, out):
    freq = scal[0]
    rows = out.shape[3]

    @pl.loop(0, outer)
    def _(k1):
        @pl.loop(0, rows // 32)
        def _(c):
            base = pl.multiple_of(c * 32, 32)
            number = k1 + outer * (base + lax.broadcasted_iota(jnp.int32, (32, LANES), 0))
            number = jnp.where(number < length // 2, number, number - length)
            fx = number.astype(jnp.float32) * (1.0 / length)
            square = fx * fx + fy2[0:1, :]
            for branch in range(2):
                wave = freq * scal[1 + branch]
                target = wave * wave - square
                turns = depth_step * jnp.sqrt(jnp.abs(target))
                live = target >= 0
                cosine, sine = circle(turns)
                decay = jnp.exp(turns * (-two_pi))
                out[branch, k1, 0, pl.ds(base, 32), :] = jnp.where(live, cosine, decay)
                out[branch, k1, 1, pl.ds(base, 32), :] = jnp.where(live, sine, 0.0)


def weight_kernel(scal, velocity, out):
    freq = scal[0]
    rows, width = velocity.shape

    @pl.loop(0, rows // ROWS)
    def _(c):
        at = pl.ds(pl.multiple_of(c * ROWS, ROWS), ROWS)
        for j in range(width // 512):
            cols = slice(j * 512, (j + 1) * 512)
            slowness = 1.0 / velocity[at, cols]
            upper = jnp.clip((slowness - scal[1]) / (scal[2] - scal[1]), 0.0, 1.0)
            for branch, weight in enumerate((1.0 - upper, upper)):
                cosine, sine = circle(depth_step * freq * (slowness - scal[1 + branch]))
                out[branch, 0, at, cols] = weight * cosine
                out[branch, 1, at, cols] = weight * sine


def row_out(mat, work, out):
    outer, rows, double = work.shape
    inner = double // 2

    @pl.loop(0, outer // 2)
    def _(g):
        x = work[pl.ds(g * 2, 2)].reshape(2 * rows, double)
        y = product(halves(x), (mat[0], mat[1])).reshape(2, rows, double)
        for j in range(2):
            out[g * 2 + j, 0] = y[j, :, :inner]
            out[g * 2 + j, 1] = y[j, :, inner:]


def twiddled(real, imag, tw, k):
    c, s = tw[k, 0], tw[k, 1]
    return real * c - imag * s, real * s + imag * c


def conj_twiddled(real, imag, c, s):
    return real * c + imag * s, imag * c - real * s


def first_kernel(field, mat, tw, out, work):
    outer, rows, double = work.shape
    inner = double // 2

    @pl.loop(0, rows // ROWS)
    def _(c):
        at = pl.ds(pl.multiple_of(c * ROWS, ROWS), ROWS)
        real = [field[0, at, a * inner : (a + 1) * inner] for a in range(outer)]
        imag = [field[1, at, a * inner : (a + 1) * inner] for a in range(outer)]
        real, imag = small_fft(real, imag, -1)
        for k in range(outer):
            work[k, at, :inner], work[k, at, inner:] = twiddled(real[k], imag[k], tw, k)

    row_out(mat, work, out)


def column_forward_kernel(got, mat, tw, out, work):
    outer, _, rows, lanes = got.shape

    @pl.loop(0, rows // ROWS)
    def _(c):
        base = pl.multiple_of(c * ROWS, ROWS)
        at = pl.ds(base, ROWS)
        real = [got[a, 0, at, :] for a in range(outer)]
        imag = [got[a, 1, at, :] for a in range(outer)]
        real, imag = small_fft(real, imag, -1)
        for k in range(outer):
            cos, sin = tw[k, 0, at, :], tw[k, 1, at, :]
            work[k, 0, at, :] = real[k] * cos - imag[k] * sin
            work[k, 1, at, :] = real[k] * sin + imag[k] * cos

    @pl.loop(0, outer // 2)
    def _(g):
        x = [work[g * 2 + j].reshape(2 * rows, lanes) for j in range(2)]
        y = product((mat[0], mat[1]), halves(jnp.concatenate(x, axis=1)))
        for j in range(2):
            out[g * 2 + j] = y[:, j * lanes : (j + 1) * lanes].reshape(2, rows, lanes)


def column_back_kernel(spec, shift, mat, tw, out, work):
    outer, _, rows, lanes = spec.shape

    @pl.loop(0, outer // 2)
    def _(g):
        parts = []
        for j in range(2):
            k = g * 2 + j
            sr, si = spec[k, 0], spec[k, 1]
            er, ei = shift[k, 0], shift[k, 1]
            parts.append(jnp.concatenate([sr * er - si * ei, sr * ei + si * er], axis=0))
        y = product((mat[0], mat[1]), halves(jnp.concatenate(parts, axis=1)))
        for j in range(2):
            k = g * 2 + j
            z = y[:, j * lanes : (j + 1) * lanes]
            work[k, 0], work[k, 1] = conj_twiddled(z[:rows], z[rows:], tw[k, 0], tw[k, 1])

    @pl.loop(0, rows // ROWS)
    def _(c):
        at = pl.ds(pl.multiple_of(c * ROWS, ROWS), ROWS)
        real = [work[k, 0, at, :] for k in range(outer)]
        imag = [work[k, 1, at, :] for k in range(outer)]
        real, imag = small_fft(real, imag, 1)
        for a in range(outer):
            out[a, 0, at, :] = real[a]
            out[a, 1, at, :] = imag[a]


def row_back(got, mat, tw, work):
    outer, rows, double = work.shape
    inner = double // 2

    @pl.loop(0, outer // 2)
    def _(g):
        x = [jnp.concatenate([got[g * 2 + j, 0], got[g * 2 + j, 1]], axis=1) for j in range(2)]
        y = product(halves(jnp.concatenate(x, axis=0)), (mat[0], mat[1])).reshape(2, rows // ROWS, ROWS, double)
        for j in range(2):
            k = g * 2 + j
            c, s = tw[k, 0][None], tw[k, 1][None]
            real, imag = conj_twiddled(y[j, :, :, :inner], y[j, :, :, inner:], c, s)
            work[k, :, :inner] = real.reshape(rows, inner)
            work[k, :, inner:] = imag.reshape(rows, inner)


def row_back_kernel(got, weight, mat, tw, out, work):
    outer, rows, double = work.shape
    inner = double // 2
    row_back(got, mat, tw, work)

    @pl.loop(0, rows // ROWS)
    def _(c):
        at = pl.ds(pl.multiple_of(c * ROWS, ROWS), ROWS)
        real = [work[k, at, :inner] for k in range(outer)]
        imag = [work[k, at, inner:] for k in range(outer)]
        real, imag = small_fft(real, imag, 1)
        for a in range(outer):
            cols = slice(a * inner, (a + 1) * inner)
            wr, wi = weight[0, at, cols], weight[1, at, cols]
            out[0, at, cols] = real[a] * wr - imag[a] * wi
            out[1, at, cols] = real[a] * wi + imag[a] * wr


def row_join_kernel(last, got, weight, part, mat, tw, mat_next, out, work):
    outer, rows, double = work.shape
    inner = double // 2
    row_back(got, mat, tw, work)

    @pl.loop(0, rows // ROWS)
    def _(c):
        at = pl.ds(pl.multiple_of(c * ROWS, ROWS), ROWS)
        real = [work[k, at, :inner] for k in range(outer)]
        imag = [work[k, at, inner:] for k in range(outer)]
        real, imag = small_fft(real, imag, 1)
        new_real, new_imag = [], []
        for a in range(outer):
            cols = slice(a * inner, (a + 1) * inner)
            wr, wi = weight[0, at, cols], weight[1, at, cols]
            new_real.append(part[0, at, cols] + (real[a] * wr - imag[a] * wi))
            new_imag.append(part[1, at, cols] + (real[a] * wi + imag[a] * wr))
        if last:
            for a in range(outer):
                cols = slice(a * inner, (a + 1) * inner)
                out[0, at, cols] = new_real[a]
                out[1, at, cols] = new_imag[a]
        else:
            real, imag = small_fft(new_real, new_imag, -1)
            for k in range(outer):
                work[k, at, :inner], work[k, at, inner:] = twiddled(real[k], imag[k], tw, k)

    if not last:
        row_out(mat_next, work, out)


def call(body, shape, work, micros, *operands, scalars=0):
    in_specs = [pl.BlockSpec(memory_space=pltpu.SMEM)] * scalars
    in_specs += [pl.BlockSpec(memory_space=pltpu.VMEM)] * (len(operands) - scalars)
    return pl.pallas_call(
        body,
        out_shape=jax.ShapeDtypeStruct(shape, jnp.float32),
        in_specs=in_specs,
        out_specs=pl.BlockSpec(memory_space=pltpu.VMEM),
        scratch_shapes=[pltpu.VMEM(work, jnp.float32)] if work else [],
        compiler_params=pltpu.CompilerParams(vmem_limit_bytes=VMEM_LIMIT),
        cost_estimate=pl.CostEstimate(flops=int(micros * 4e8), bytes_accessed=int(micros * 3e6), transcendentals=0),
    )(*operands)


def shards(wavefield, freqs, velocity, ref_slow):
    slabs = lax.axis_size("slab")
    slab_index = lax.axis_index("slab")
    rows = wavefield.shape[2]
    width_x = rows * slabs
    width_y = wavefield.shape[3]
    columns = width_y // slabs
    depth = ref_slow.shape[0]
    across = (slabs, 2, rows, columns)
    row_fwd = matrix_of(columns, width_y, -1, False)
    row_inv = matrix_of(columns, width_y, 1, False)
    col_fwd = matrix_of(rows, width_x, -1, True)
    col_inv = matrix_of(rows, width_x, 1, True)
    row_tw = twiddle_table(slabs, columns, False)
    col_tw = twiddle_table(slabs, rows, True)
    row_work = (slabs, rows, 2 * columns)

    number = slab_index + slabs * jnp.arange(columns, dtype=jnp.int32)
    number = jnp.where(number < width_y // 2, number, number - width_y)
    along_y = number.astype(jnp.float32) / width_y
    fy2 = jnp.broadcast_to((along_y * along_y)[None, :], (ROWS, columns))

    def exchange(x):
        return lax.all_to_all(x, "slab", split_axis=0, concat_axis=0, tiled=True)

    freq_count = lax.axis_size("freq")
    tiles = jnp.broadcast_to(velocity[None], (freq_count,) + velocity.shape)
    tiles = lax.all_to_all(tiles, "freq", split_axis=0, concat_axis=0, tiled=True)

    part_send = call(first_kernel, across, row_work, 4, wavefield[:, 0], row_fwd, row_tw)
    for level in range(depth):
        last = level == depth - 1
        scal = jnp.concatenate([freqs, ref_slow[level]])
        got = exchange(part_send)
        shift = call(
            functools.partial(spread_kernel, slabs, width_x), (2,) + across, None, 8, scal, fy2, scalars=1
        )
        tile = jnp.concatenate([tiles[i, level] for i in range(freq_count)], axis=1)
        weight = call(weight_kernel, (2, 2, rows, width_y), None, 8, scal, tile, scalars=1)
        spec = call(column_forward_kernel, across, across, 4, got, col_fwd, col_tw)
        back = []
        for branch in range(2):
            sent = call(column_back_kernel, across, across, 4, spec, shift[branch], col_inv, col_tw)
            back.append(exchange(sent))
        part = call(row_back_kernel, (2, rows, width_y), row_work, 4, back[0], weight[0], row_inv, row_tw)
        part_send = call(
            functools.partial(row_join_kernel, last),
            (2, rows, width_y) if last else across,
            row_work, 5, back[1], weight[1], part, row_inv, row_tw, row_fwd,
        )
    return part_send[:, None]


def solution(mesh):
    slabs = mesh.shape["slab"]

    def program(wavefield, freqs, velocity, ref_slow):
        width_x, width_y = wavefield.shape[2:]
        whole_tiles = (
            width_y // slabs == LANES
            and width_x // slabs == LANES
            and wavefield.shape[1] == mesh.shape["freq"]
        )
        return jax.shard_map(
            shards if whole_tiles else shards_generic,
            mesh=mesh,
            in_specs=(P(None, "freq", "slab", None), P("freq"), P(None, "slab", "freq"), P()),
            out_specs=P(None, "freq", "slab", None),
            check_vma=False,
        )(wavefield, freqs, velocity, ref_slow)

    return program
```

```python
import functools
import math

import jax
import jax.numpy as jnp
import numpy as np
from jax import lax
from jax.experimental import pallas as pl
from jax.experimental.pallas import tpu as pltpu
from jax.sharding import PartitionSpec as P

two_pi = 2.0 * math.pi
depth_step = 2.0


def dft_matrix(length, sign):
    index = jnp.arange(length, dtype=jnp.int32)
    product = index[:, None] * index[None, :] % length
    angle = sign * two_pi / length * product.astype(jnp.float32)
    scale = 1.0 / math.sqrt(length)
    return (jnp.cos(angle) * scale, jnp.sin(angle) * scale)


def twiddle(outer, inner, sign):
    length = outer * inner
    product = (
        jnp.arange(outer, dtype=jnp.int32)[:, None]
        * jnp.arange(inner, dtype=jnp.int32)[None, :]
        % length
    )
    angle = sign * two_pi / length * product.astype(jnp.float32)
    return (jnp.cos(angle), jnp.sin(angle))


def complex_mix(form, mat_real, mat_imag, data_real, data_imag):

    def product(matrix, data):
        return jnp.einsum(form, matrix, data, precision=lax.Precision.HIGHEST)

    return (
        product(mat_real, data_real) - product(mat_imag, data_imag),
        product(mat_real, data_imag) + product(mat_imag, data_real),
    )


def transform(real, imag, trailing, sign):
    length = real.shape[-2] if trailing else real.shape[-1]
    inner = min(length, 128)
    outer = length // inner
    outer_real, outer_imag = dft_matrix(outer, sign)
    inner_real, inner_imag = dft_matrix(inner, sign)
    turn_real, turn_imag = twiddle(outer, inner, sign)
    if trailing:
        leading = real.shape[:-2]
        tail = real.shape[-1:]
        form_outer = "ka,...abm->...kbm"
        form_inner = "bj,...kbm->...kjm"
        turn_real = turn_real[:, :, None]
        turn_imag = turn_imag[:, :, None]
    else:
        leading = real.shape[:-1]
        tail = ()
        form_outer = "ka,...ab->...kb"
        form_inner = "bj,...kb->...kj"
    split_shape = leading + (outer, inner) + tail
    real = real.reshape(split_shape)
    imag = imag.reshape(split_shape)
    if sign < 0:
        real, imag = complex_mix(form_outer, outer_real, outer_imag, real, imag)
        real, imag = (real * turn_real - imag * turn_imag, real * turn_imag + imag * turn_real)
        real, imag = complex_mix(form_inner, inner_real, inner_imag, real, imag)
    else:
        real, imag = complex_mix(form_inner, inner_real, inner_imag, real, imag)
        real, imag = (real * turn_real - imag * turn_imag, real * turn_imag + imag * turn_real)
        real, imag = complex_mix(form_outer, outer_real, outer_imag, real, imag)
    joined = leading + (length,) + tail
    return (real.reshape(joined), imag.reshape(joined))


def wave_numbers(positions, length):
    inner = min(length, 128)
    outer = length // inner
    number = positions // inner + outer * (positions % inner)
    number = jnp.where(number < length // 2, number, number - length)
    return number.astype(jnp.float32) / length


def forward_x(items):
    real, imag = transform(items[0], items[1], True, -1)
    return jnp.stack((real, imag))


def inverse_y(items):
    real, imag = transform(items[:, 0], items[:, 1], False, 1)
    return jnp.stack((real, imag), axis=1)


def shards_generic(wavefield, freqs, velocity, ref_slow):
    slabs = lax.axis_size("slab")
    slab_index = lax.axis_index("slab")
    rows = wavefield.shape[2]
    width_x = rows * slabs
    width_y = wavefield.shape[3]
    columns = width_y // slabs
    depth = ref_slow.shape[0]
    along_x = wave_numbers(jnp.arange(width_x, dtype=jnp.int32), width_x)
    along_y = wave_numbers(slab_index * columns + jnp.arange(columns, dtype=jnp.int32), width_y)
    square = along_x[:, None] ** 2 + along_y[None, :] ** 2
    freq_col = freqs[:, None, None]

    def advance(level, field):
        local_tile = lax.dynamic_index_in_dim(velocity, level, 0, keepdims=False)
        tile = lax.all_gather(local_tile, "freq", axis=1, tiled=True)
        real, imag = transform(field[0], field[1], False, -1)
        spectrum = forward_x(
            lax.all_to_all(jnp.stack((real, imag)), "slab", split_axis=3, concat_axis=2, tiled=True)
        )
        slow_pair = lax.dynamic_index_in_dim(ref_slow, level, 0, keepdims=False)
        slowness = 1.0 / tile
        upper_weight = jnp.clip((slowness - slow_pair[0]) / (slow_pair[1] - slow_pair[0]), 0.0, 1.0)
        weights = [1.0 - upper_weight, upper_weight]
        shifted = []
        for branch in range(2):
            target = (freq_col * slow_pair[branch]) ** 2 - square[None]
            angle = two_pi * depth_step * jnp.sqrt(jnp.abs(target))
            live = target >= 0
            prop_real = jnp.where(live, jnp.cos(angle), jnp.exp(-angle))
            prop_imag = jnp.where(live, jnp.sin(angle), jnp.zeros_like(angle))
            spec_real = spectrum[0] * prop_real - spectrum[1] * prop_imag
            spec_imag = spectrum[0] * prop_imag + spectrum[1] * prop_real
            back_real, back_imag = transform(spec_real, spec_imag, True, 1)
            shifted.append(jnp.stack((back_real, back_imag)))
        pieces = []
        for branch in range(2):
            moved = lax.all_to_all(shifted[branch], "slab", split_axis=2, concat_axis=3, tiled=True)
            pieces.append(inverse_y(moved[None])[0])
        spatial = jnp.stack(pieces)
        new_real = jnp.zeros_like(field[0])
        new_imag = jnp.zeros_like(field[1])
        for branch in range(2):
            theta = two_pi * depth_step * freq_col * (slowness - slow_pair[branch])[None]
            weight = weights[branch][None]
            cosine = jnp.cos(theta)
            sine = jnp.sin(theta)
            part_real = spatial[branch, 0]
            part_imag = spatial[branch, 1]
            new_real = new_real + weight * (cosine * part_real - sine * part_imag)
            new_imag = new_imag + weight * (cosine * part_imag + sine * part_real)
        return jnp.stack((new_real, new_imag))

    return lax.fori_loop(0, depth, advance, wavefield)


LANES = 128
ROWS = 8
VMEM_LIMIT = 56 * 2**20


def turn(numerator, denominator, sign):
    angle = sign * 2.0 * np.pi * ((numerator % denominator) / denominator)
    return (np.cos(angle), np.sin(angle))


def times(real, imag, c, s):
    if abs(s) < 1e-12:
        return (real, imag) if c > 0 else (-real, -imag)
    if abs(c) < 1e-12:
        return (-imag, real) if s > 0 else (imag, -real)
    if abs(abs(c) - abs(s)) < 1e-12:
        k = float(abs(c))
        a, b = (k if c > 0 else -k), (s > 0) == (c > 0)
        if b:
            return ((real - imag) * a, (real + imag) * a)
        return ((real + imag) * a, (imag - real) * a)
    c, s = float(c), float(s)
    return (real * c - imag * s, real * s + imag * c)


def small_fft(real, imag, sign):
    count = len(real)
    if count == 1:
        return real, imag
    er, ei = small_fft(real[0::2], imag[0::2], sign)
    odd_r, odd_i = small_fft(real[1::2], imag[1::2], sign)
    low, high = [], []
    for k in range(count // 2):
        tr, ti = times(odd_r[k], odd_i[k], *turn(k, count, sign))
        low.append((er[k] + tr, ei[k] + ti))
        high.append((er[k] - tr, ei[k] - ti))
    both = low + high
    return [v[0] for v in both], [v[1] for v in both]


def halves(x):
    high = x.astype(jnp.bfloat16)
    low = (x - high.astype(jnp.float32)).astype(jnp.bfloat16)
    return high, low


def product(a, b):
    def dot(p, q):
        return jnp.dot(p, q, preferred_element_type=jnp.float32)

    return dot(a[0], b[0]) + (dot(a[0], b[1]) + dot(a[1], b[0]))


def matrix_of(inner, length, sign, left):
    index = np.arange(inner)
    angle = sign * 2.0 * np.pi * ((index[:, None] * index[None, :]) % inner) / inner
    c = np.cos(angle) / np.sqrt(length)
    s = np.sin(angle) / np.sqrt(length)
    full = np.block([[c, -s], [s, c]]) if left else np.block([[c, s], [-s, c]])
    full = full.astype(np.float32)
    high = full.astype(jnp.bfloat16)
    low = (full - high.astype(np.float32)).astype(jnp.bfloat16)
    return np.stack([high, low])


def twiddle_table(outer, inner, rows):
    c, s = turn(np.arange(outer)[:, None] * np.arange(inner)[None, :], outer * inner, -1)
    both = np.stack([c, s], axis=1).astype(np.float32)
    if rows:
        return np.ascontiguousarray(np.broadcast_to(both[:, :, :, None], (outer, 2, inner, LANES)))
    return np.ascontiguousarray(np.broadcast_to(both[:, :, None, :], (outer, 2, ROWS, inner)))


def cosine_terms():
    z = 0.125 + 0.125 * np.cos(np.pi * (np.arange(400) + 0.5) / 400)
    r = np.sqrt(z)

    def fit(values, degree):
        poly = np.polynomial.Chebyshev.fit(z, values, degree, domain=[0.0, 0.25])
        poly = poly.convert(kind=np.polynomial.Polynomial)
        return [float(np.float32(v)) for v in poly.coef]

    return fit(np.cos(2 * np.pi * r), 8), fit(np.sin(2 * np.pi * r) / r, 7)


COS_TERMS, SIN_TERMS = cosine_terms()


def horner(terms, z):
    value = z * terms[-1] + terms[-2]
    for term in terms[-3::-1]:
        value = value * z + term
    return value


def circle(turns):
    rest = turns - jnp.round(turns)
    z = rest * rest
    return horner(COS_TERMS, z), rest * horner(SIN_TERMS, z)


def spread_kernel(outer, length, scal, fy2, *outs):
    freq = scal[0]
    rows = outs[0].shape[2]

    @pl.loop(0, outer)
    def _(k1):
        @pl.loop(0, rows // 32)
        def _(c):
            base = pl.multiple_of(c * 32, 32)
            number = k1 + outer * (base + lax.broadcasted_iota(jnp.int32, (32, LANES), 0))
            number = jnp.where(number < length // 2, number, number - length)
            fx = number.astype(jnp.float32) * (1.0 / length)
            square = fx * fx + fy2[0:1, :]
            for branch in range(2):
                wave = freq * scal[1 + branch]
                target = wave * wave - square
                turns = depth_step * jnp.sqrt(jnp.abs(target))
                live = target >= 0
                cosine, sine = circle(turns)
                decay = jnp.exp(turns * (-two_pi))
                outs[branch][k1, 0, pl.ds(base, 32), :] = jnp.where(live, cosine, decay)
                outs[branch][k1, 1, pl.ds(base, 32), :] = jnp.where(live, sine, 0.0)


def weight_kernel(scal, order, *refs):
    tiles, outs = refs[:-2], refs[-2:]
    freq = scal[0]
    rows, part = tiles[0].shape
    width = part * len(tiles)

    @pl.loop(0, rows // ROWS)
    def _(c):
        at = pl.ds(pl.multiple_of(c * ROWS, ROWS), ROWS)
        for j in range(width // 512):
            cols = slice(j * 512, (j + 1) * 512)
            first = j * 512 // part
            inside = slice(j * 512 - first * part, (j + 1) * 512 - first * part)
            here, there = tiles[first][at, inside], tiles[1 - first][at, inside]
            slowness = 1.0 / jnp.where(order[0] == 0, here, there)
            upper = jnp.clip((slowness - scal[1]) / (scal[2] - scal[1]), 0.0, 1.0)
            for branch, weight in enumerate((1.0 - upper, upper)):
                cosine, sine = circle(depth_step * freq * (slowness - scal[1 + branch]))
                outs[branch][0, at, cols] = weight * cosine
                outs[branch][1, at, cols] = weight * sine


def row_out(mat, work, out):
    outer, rows, double = work.shape
    inner = double // 2

    @pl.loop(0, outer // 2)
    def _(g):
        x = work[pl.ds(g * 2, 2)].reshape(2 * rows, double)
        y = product(halves(x), (mat[0], mat[1])).reshape(2, rows, double)
        for j in range(2):
            out[g * 2 + j, 0] = y[j, :, :inner]
            out[g * 2 + j, 1] = y[j, :, inner:]


def twiddled(real, imag, tw, k):
    c, s = tw[k, 0], tw[k, 1]
    return real * c - imag * s, real * s + imag * c


def conj_twiddled(real, imag, c, s):
    return real * c + imag * s, imag * c - real * s


def first_kernel(field, mat, tw, out, work):
    outer, rows, double = work.shape
    inner = double // 2

    @pl.loop(0, rows // ROWS)
    def _(c):
        at = pl.ds(pl.multiple_of(c * ROWS, ROWS), ROWS)
        real = [field[0, at, a * inner : (a + 1) * inner] for a in range(outer)]
        imag = [field[1, at, a * inner : (a + 1) * inner] for a in range(outer)]
        real, imag = small_fft(real, imag, -1)
        for k in range(outer):
            work[k, at, :inner], work[k, at, inner:] = twiddled(real[k], imag[k], tw, k)

    row_out(mat, work, out)


def column_forward_kernel(got, mat, tw, out, work):
    outer, _, rows, lanes = got.shape

    @pl.loop(0, rows // ROWS)
    def _(c):
        base = pl.multiple_of(c * ROWS, ROWS)
        at = pl.ds(base, ROWS)
        real = [got[a, 0, at, :] for a in range(outer)]
        imag = [got[a, 1, at, :] for a in range(outer)]
        real, imag = small_fft(real, imag, -1)
        for k in range(outer):
            cos, sin = tw[k, 0, at, :], tw[k, 1, at, :]
            work[k, 0, at, :] = real[k] * cos - imag[k] * sin
            work[k, 1, at, :] = real[k] * sin + imag[k] * cos

    @pl.loop(0, outer // 2)
    def _(g):
        x = [work[g * 2 + j].reshape(2 * rows, lanes) for j in range(2)]
        y = product((mat[0], mat[1]), halves(jnp.concatenate(x, axis=1)))
        for j in range(2):
            out[g * 2 + j] = y[:, j * lanes : (j + 1) * lanes].reshape(2, rows, lanes)


def column_back_kernel(spec, shift, mat, tw, out, work):
    outer, _, rows, lanes = spec.shape

    @pl.loop(0, outer // 2)
    def _(g):
        parts = []
        for j in range(2):
            k = g * 2 + j
            sr, si = spec[k, 0], spec[k, 1]
            er, ei = shift[k, 0], shift[k, 1]
            parts.append(jnp.concatenate([sr * er - si * ei, sr * ei + si * er], axis=0))
        y = product((mat[0], mat[1]), halves(jnp.concatenate(parts, axis=1)))
        for j in range(2):
            k = g * 2 + j
            z = y[:, j * lanes : (j + 1) * lanes]
            work[k, 0], work[k, 1] = conj_twiddled(z[:rows], z[rows:], tw[k, 0], tw[k, 1])

    @pl.loop(0, rows // ROWS)
    def _(c):
        at = pl.ds(pl.multiple_of(c * ROWS, ROWS), ROWS)
        real = [work[k, 0, at, :] for k in range(outer)]
        imag = [work[k, 1, at, :] for k in range(outer)]
        real, imag = small_fft(real, imag, 1)
        for a in range(outer):
            out[a, 0, at, :] = real[a]
            out[a, 1, at, :] = imag[a]


def row_back(got, mat, tw, work):
    outer, rows, double = work.shape
    inner = double // 2

    @pl.loop(0, outer // 2)
    def _(g):
        x = [jnp.concatenate([got[g * 2 + j, 0], got[g * 2 + j, 1]], axis=1) for j in range(2)]
        y = product(halves(jnp.concatenate(x, axis=0)), (mat[0], mat[1])).reshape(2, rows // ROWS, ROWS, double)
        for j in range(2):
            k = g * 2 + j
            c, s = tw[k, 0][None], tw[k, 1][None]
            real, imag = conj_twiddled(y[j, :, :, :inner], y[j, :, :, inner:], c, s)
            work[k, :, :inner] = real.reshape(rows, inner)
            work[k, :, inner:] = imag.reshape(rows, inner)


def row_back_kernel(got, weight, mat, tw, out, work):
    outer, rows, double = work.shape
    inner = double // 2
    row_back(got, mat, tw, work)

    @pl.loop(0, rows // ROWS)
    def _(c):
        at = pl.ds(pl.multiple_of(c * ROWS, ROWS), ROWS)
        real = [work[k, at, :inner] for k in range(outer)]
        imag = [work[k, at, inner:] for k in range(outer)]
        real, imag = small_fft(real, imag, 1)
        for a in range(outer):
            cols = slice(a * inner, (a + 1) * inner)
            wr, wi = weight[0, at, cols], weight[1, at, cols]
            out[0, at, cols] = real[a] * wr - imag[a] * wi
            out[1, at, cols] = real[a] * wi + imag[a] * wr


def row_join_kernel(last, got, weight, part, mat, tw, mat_next, out, work):
    outer, rows, double = work.shape
    inner = double // 2
    row_back(got, mat, tw, work)

    @pl.loop(0, rows // ROWS)
    def _(c):
        at = pl.ds(pl.multiple_of(c * ROWS, ROWS), ROWS)
        real = [work[k, at, :inner] for k in range(outer)]
        imag = [work[k, at, inner:] for k in range(outer)]
        real, imag = small_fft(real, imag, 1)
        new_real, new_imag = [], []
        for a in range(outer):
            cols = slice(a * inner, (a + 1) * inner)
            wr, wi = weight[0, at, cols], weight[1, at, cols]
            new_real.append(part[0, at, cols] + (real[a] * wr - imag[a] * wi))
            new_imag.append(part[1, at, cols] + (real[a] * wi + imag[a] * wr))
        if last:
            for a in range(outer):
                cols = slice(a * inner, (a + 1) * inner)
                out[0, at, cols] = new_real[a]
                out[1, at, cols] = new_imag[a]
        else:
            real, imag = small_fft(new_real, new_imag, -1)
            for k in range(outer):
                work[k, at, :inner], work[k, at, inner:] = twiddled(real[k], imag[k], tw, k)

    if not last:
        row_out(mat_next, work, out)


def call(body, shape, work, micros, *operands, scalars=0, outputs=1):
    in_specs = [pl.BlockSpec(memory_space=pltpu.SMEM)] * scalars
    in_specs += [pl.BlockSpec(memory_space=pltpu.VMEM)] * (len(operands) - scalars)
    result = jax.ShapeDtypeStruct(shape, jnp.float32)
    spec = pl.BlockSpec(memory_space=pltpu.VMEM)
    return pl.pallas_call(
        body,
        out_shape=result if outputs == 1 else (result,) * outputs,
        in_specs=in_specs,
        out_specs=spec if outputs == 1 else (spec,) * outputs,
        scratch_shapes=[pltpu.VMEM(work, jnp.float32)] if work else [],
        compiler_params=pltpu.CompilerParams(vmem_limit_bytes=VMEM_LIMIT),
        cost_estimate=pl.CostEstimate(flops=int(micros * 4e8), bytes_accessed=int(micros * 3e6), transcendentals=0),
    )(*operands)


def shards(wavefield, freqs, velocity, ref_slow):
    slabs = lax.axis_size("slab")
    slab_index = lax.axis_index("slab")
    rows = wavefield.shape[2]
    width_x = rows * slabs
    width_y = wavefield.shape[3]
    columns = width_y // slabs
    depth = ref_slow.shape[0]
    across = (slabs, 2, rows, columns)
    row_fwd = matrix_of(columns, width_y, -1, False)
    row_inv = matrix_of(columns, width_y, 1, False)
    col_fwd = matrix_of(rows, width_x, -1, True)
    col_inv = matrix_of(rows, width_x, 1, True)
    row_tw = twiddle_table(slabs, columns, False)
    col_tw = twiddle_table(slabs, rows, True)
    row_work = (slabs, rows, 2 * columns)

    freq_count = lax.axis_size("freq")
    group = slabs // freq_count
    run = group // freq_count
    row = lax.axis_index("freq")
    both = ("freq", "slab")
    everyone = [(y, s) for y in range(freq_count) for s in range(slabs)]

    def owner(slab):
        return (slab // run) % freq_count, (slab // group) * run + slab % run

    def device(y, g, place):
        return y * slabs + g * group + place

    members = []
    for g in range(freq_count):
        members.append([device(y, g, place) for y, place in map(owner, range(slabs))])
    here = lax.rem(slab_index, group)
    mine = (here // run) * group + row * run + lax.rem(here, run)

    def swap(x, name):
        return lax.all_to_all(x, name, split_axis=0, concat_axis=0, tiled=True)

    def exchange(x):
        return lax.all_to_all(x, both, split_axis=0, concat_axis=0, tiled=True, axis_index_groups=members)

    home = [(y * slabs + s, (s // group) * slabs + y * group + s % group) for y, s in everyone]
    group_freq = lax.ppermute(freqs, both, home)

    number = mine + slabs * jnp.arange(columns, dtype=jnp.int32)
    number = jnp.where(number < width_y // 2, number, number - width_y)
    along_y = number.astype(jnp.float32) / width_y
    fy2 = jnp.broadcast_to((along_y * along_y)[None, :], (ROWS, columns))

    part_send = call(first_kernel, across, row_work, 4, wavefield[:, 0], row_fwd, row_tw)
    sends = part_send.reshape(freq_count, freq_count, run, 2, rows, columns)
    sends = sends.swapaxes(0, 1).reshape(across)
    got = swap(swap(sends, "freq"), "slab")

    def grouped_velocity(level):
        moved = []
        for shift in range(freq_count):
            route = []
            for y, s in everyone:
                to_row, place = owner(s)
                route.append((y * slabs + s, device(to_row, (to_row + y + shift) % freq_count, place)))
            moved.append(lax.ppermute(velocity[level], both, route))
        return moved

    order = ((slab_index // group + freq_count - row) % freq_count).astype(jnp.int32)[None]

    for level in range(depth):
        last = level == depth - 1
        if level:
            got = exchange(part_send)
        with jax.named_scope(f"vel{level}"):
            tiles = grouped_velocity(level)
        scal = jnp.concatenate([group_freq, ref_slow[level]])
        shift = call(
            functools.partial(spread_kernel, slabs, width_x), across, None, 8, scal, fy2, scalars=1, outputs=2
        )
        weight = call(weight_kernel, (2, rows, width_y), None, 8, scal, order, *tiles, scalars=2, outputs=2)
        spec = call(column_forward_kernel, across, across, 7, got, col_fwd, col_tw)
        back = []
        for branch in range(2):
            sent = call(column_back_kernel, across, across, 7, spec, shift[branch], col_inv, col_tw)
            with jax.named_scope(f"back{level}_{branch}"):
                back.append(exchange(sent))
        part = call(row_back_kernel, (2, rows, width_y), row_work, 6, back[0], weight[0], row_inv, row_tw)
        part_send = call(
            functools.partial(row_join_kernel, last),
            (2, rows, width_y) if last else across,
            row_work, 9, back[1], weight[1], part, row_inv, row_tw, row_fwd,
        )
    leave = []
    for y, s in everyone:
        to_row, place = owner(s)
        leave.append((device(to_row, y, place), y * slabs + s))
    return lax.ppermute(part_send, both, leave)[:, None]


def solution(mesh):
    slabs = mesh.shape["slab"]

    def program(wavefield, freqs, velocity, ref_slow):
        width_x, width_y = wavefield.shape[2:]
        whole_tiles = (
            width_y // slabs == LANES
            and width_x // slabs == LANES
            and wavefield.shape[1] == mesh.shape["freq"] == 2
            and slabs % 4 == 0
        )
        return jax.shard_map(
            shards if whole_tiles else shards_generic,
            mesh=mesh,
            in_specs=(P(None, "freq", "slab", None), P("freq"), P(None, "slab", "freq"), P()),
            out_specs=P(None, "freq", "slab", None),
            check_vma=False,
        )(wavefield, freqs, velocity, ref_slow)

    return program
```

```python
import functools
import math

import jax
import jax.numpy as jnp
import numpy as np
from jax import lax
from jax.experimental import pallas as pl
from jax.experimental.pallas import tpu as pltpu
from jax.sharding import PartitionSpec as P

two_pi = 2.0 * math.pi
depth_step = 2.0


def dft_matrix(length, sign):
    index = jnp.arange(length, dtype=jnp.int32)
    product = index[:, None] * index[None, :] % length
    angle = sign * two_pi / length * product.astype(jnp.float32)
    scale = 1.0 / math.sqrt(length)
    return (jnp.cos(angle) * scale, jnp.sin(angle) * scale)


def twiddle(outer, inner, sign):
    length = outer * inner
    product = (
        jnp.arange(outer, dtype=jnp.int32)[:, None]
        * jnp.arange(inner, dtype=jnp.int32)[None, :]
        % length
    )
    angle = sign * two_pi / length * product.astype(jnp.float32)
    return (jnp.cos(angle), jnp.sin(angle))


def complex_mix(form, mat_real, mat_imag, data_real, data_imag):

    def product(matrix, data):
        return jnp.einsum(form, matrix, data, precision=lax.Precision.HIGHEST)

    return (
        product(mat_real, data_real) - product(mat_imag, data_imag),
        product(mat_real, data_imag) + product(mat_imag, data_real),
    )


def transform(real, imag, trailing, sign):
    length = real.shape[-2] if trailing else real.shape[-1]
    inner = min(length, 128)
    outer = length // inner
    outer_real, outer_imag = dft_matrix(outer, sign)
    inner_real, inner_imag = dft_matrix(inner, sign)
    turn_real, turn_imag = twiddle(outer, inner, sign)
    if trailing:
        leading = real.shape[:-2]
        tail = real.shape[-1:]
        form_outer = "ka,...abm->...kbm"
        form_inner = "bj,...kbm->...kjm"
        turn_real = turn_real[:, :, None]
        turn_imag = turn_imag[:, :, None]
    else:
        leading = real.shape[:-1]
        tail = ()
        form_outer = "ka,...ab->...kb"
        form_inner = "bj,...kb->...kj"
    split_shape = leading + (outer, inner) + tail
    real = real.reshape(split_shape)
    imag = imag.reshape(split_shape)
    if sign < 0:
        real, imag = complex_mix(form_outer, outer_real, outer_imag, real, imag)
        real, imag = (real * turn_real - imag * turn_imag, real * turn_imag + imag * turn_real)
        real, imag = complex_mix(form_inner, inner_real, inner_imag, real, imag)
    else:
        real, imag = complex_mix(form_inner, inner_real, inner_imag, real, imag)
        real, imag = (real * turn_real - imag * turn_imag, real * turn_imag + imag * turn_real)
        real, imag = complex_mix(form_outer, outer_real, outer_imag, real, imag)
    joined = leading + (length,) + tail
    return (real.reshape(joined), imag.reshape(joined))


def wave_numbers(positions, length):
    inner = min(length, 128)
    outer = length // inner
    number = positions // inner + outer * (positions % inner)
    number = jnp.where(number < length // 2, number, number - length)
    return number.astype(jnp.float32) / length


def forward_x(items):
    real, imag = transform(items[0], items[1], True, -1)
    return jnp.stack((real, imag))


def inverse_y(items):
    real, imag = transform(items[:, 0], items[:, 1], False, 1)
    return jnp.stack((real, imag), axis=1)


def shards_generic(wavefield, freqs, velocity, ref_slow):
    slabs = lax.axis_size("slab")
    slab_index = lax.axis_index("slab")
    rows = wavefield.shape[2]
    width_x = rows * slabs
    width_y = wavefield.shape[3]
    columns = width_y // slabs
    depth = ref_slow.shape[0]
    along_x = wave_numbers(jnp.arange(width_x, dtype=jnp.int32), width_x)
    along_y = wave_numbers(slab_index * columns + jnp.arange(columns, dtype=jnp.int32), width_y)
    square = along_x[:, None] ** 2 + along_y[None, :] ** 2
    freq_col = freqs[:, None, None]

    def advance(level, field):
        local_tile = lax.dynamic_index_in_dim(velocity, level, 0, keepdims=False)
        tile = lax.all_gather(local_tile, "freq", axis=1, tiled=True)
        real, imag = transform(field[0], field[1], False, -1)
        spectrum = forward_x(
            lax.all_to_all(jnp.stack((real, imag)), "slab", split_axis=3, concat_axis=2, tiled=True)
        )
        slow_pair = lax.dynamic_index_in_dim(ref_slow, level, 0, keepdims=False)
        slowness = 1.0 / tile
        upper_weight = jnp.clip((slowness - slow_pair[0]) / (slow_pair[1] - slow_pair[0]), 0.0, 1.0)
        weights = [1.0 - upper_weight, upper_weight]
        shifted = []
        for branch in range(2):
            target = (freq_col * slow_pair[branch]) ** 2 - square[None]
            angle = two_pi * depth_step * jnp.sqrt(jnp.abs(target))
            live = target >= 0
            prop_real = jnp.where(live, jnp.cos(angle), jnp.exp(-angle))
            prop_imag = jnp.where(live, jnp.sin(angle), jnp.zeros_like(angle))
            spec_real = spectrum[0] * prop_real - spectrum[1] * prop_imag
            spec_imag = spectrum[0] * prop_imag + spectrum[1] * prop_real
            back_real, back_imag = transform(spec_real, spec_imag, True, 1)
            shifted.append(jnp.stack((back_real, back_imag)))
        pieces = []
        for branch in range(2):
            moved = lax.all_to_all(shifted[branch], "slab", split_axis=2, concat_axis=3, tiled=True)
            pieces.append(inverse_y(moved[None])[0])
        spatial = jnp.stack(pieces)
        new_real = jnp.zeros_like(field[0])
        new_imag = jnp.zeros_like(field[1])
        for branch in range(2):
            theta = two_pi * depth_step * freq_col * (slowness - slow_pair[branch])[None]
            weight = weights[branch][None]
            cosine = jnp.cos(theta)
            sine = jnp.sin(theta)
            part_real = spatial[branch, 0]
            part_imag = spatial[branch, 1]
            new_real = new_real + weight * (cosine * part_real - sine * part_imag)
            new_imag = new_imag + weight * (cosine * part_imag + sine * part_real)
        return jnp.stack((new_real, new_imag))

    return lax.fori_loop(0, depth, advance, wavefield)


LANES = 128
ROWS = 8
VMEM_LIMIT = 56 * 2**20


def turn(numerator, denominator, sign):
    angle = sign * 2.0 * np.pi * ((numerator % denominator) / denominator)
    return (np.cos(angle), np.sin(angle))


def times(real, imag, c, s):
    if abs(s) < 1e-12:
        return (real, imag) if c > 0 else (-real, -imag)
    if abs(c) < 1e-12:
        return (-imag, real) if s > 0 else (imag, -real)
    if abs(abs(c) - abs(s)) < 1e-12:
        k = float(abs(c))
        a, b = (k if c > 0 else -k), (s > 0) == (c > 0)
        if b:
            return ((real - imag) * a, (real + imag) * a)
        return ((real + imag) * a, (imag - real) * a)
    c, s = float(c), float(s)
    return (real * c - imag * s, real * s + imag * c)


def small_fft(real, imag, sign):
    count = len(real)
    if count == 1:
        return real, imag
    er, ei = small_fft(real[0::2], imag[0::2], sign)
    odd_r, odd_i = small_fft(real[1::2], imag[1::2], sign)
    low, high = [], []
    for k in range(count // 2):
        tr, ti = times(odd_r[k], odd_i[k], *turn(k, count, sign))
        low.append((er[k] + tr, ei[k] + ti))
        high.append((er[k] - tr, ei[k] - ti))
    both = low + high
    return [v[0] for v in both], [v[1] for v in both]


def halves(x):
    high = x.astype(jnp.bfloat16)
    low = (x - high.astype(jnp.float32)).astype(jnp.bfloat16)
    return high, low


def product(a, b):
    def dot(p, q):
        return jnp.dot(p, q, preferred_element_type=jnp.float32)

    return dot(a[0], b[0]) + (dot(a[0], b[1]) + dot(a[1], b[0]))


def matrix_of(inner, length, sign, left):
    index = np.arange(inner)
    angle = sign * 2.0 * np.pi * ((index[:, None] * index[None, :]) % inner) / inner
    c = np.cos(angle) / np.sqrt(length)
    s = np.sin(angle) / np.sqrt(length)
    full = np.block([[c, -s], [s, c]]) if left else np.block([[c, s], [-s, c]])
    full = full.astype(np.float32)
    high = full.astype(jnp.bfloat16)
    low = (full - high.astype(np.float32)).astype(jnp.bfloat16)
    return np.stack([high, low])


def twiddle_table(outer, inner, rows):
    c, s = turn(np.arange(outer)[:, None] * np.arange(inner)[None, :], outer * inner, -1)
    both = np.stack([c, s], axis=1).astype(np.float32)
    if rows:
        return np.ascontiguousarray(np.broadcast_to(both[:, :, :, None], (outer, 2, inner, LANES)))
    return np.ascontiguousarray(np.broadcast_to(both[:, :, None, :], (outer, 2, ROWS, inner)))


def cosine_terms():
    z = 0.125 + 0.125 * np.cos(np.pi * (np.arange(400) + 0.5) / 400)
    r = np.sqrt(z)

    def fit(values, degree):
        poly = np.polynomial.Chebyshev.fit(z, values, degree, domain=[0.0, 0.25])
        poly = poly.convert(kind=np.polynomial.Polynomial)
        return [float(np.float32(v)) for v in poly.coef]

    return fit(np.cos(2 * np.pi * r), 8), fit(np.sin(2 * np.pi * r) / r, 7)


COS_TERMS, SIN_TERMS = cosine_terms()


def horner(terms, z):
    value = z * terms[-1] + terms[-2]
    for term in terms[-3::-1]:
        value = value * z + term
    return value


def circle(turns):
    rest = turns - jnp.round(turns)
    z = rest * rest
    return horner(COS_TERMS, z), rest * horner(SIN_TERMS, z)


def spread_kernel(outer, length, scal, fy2, *outs):
    freq = scal[0]
    rows = outs[0].shape[2]

    @pl.loop(0, outer)
    def _(k1):
        @pl.loop(0, rows // 32)
        def _(c):
            base = pl.multiple_of(c * 32, 32)
            number = k1 + outer * (base + lax.broadcasted_iota(jnp.int32, (32, LANES), 0))
            number = jnp.where(number < length // 2, number, number - length)
            fx = number.astype(jnp.float32) * (1.0 / length)
            square = fx * fx + fy2[0:1, :]
            for branch in range(2):
                wave = freq * scal[1 + branch]
                target = wave * wave - square
                turns = depth_step * jnp.sqrt(jnp.abs(target))
                live = target >= 0
                cosine, sine = circle(turns)
                decay = jnp.exp(turns * (-two_pi))
                outs[branch][k1, 0, pl.ds(base, 32), :] = jnp.where(live, cosine, decay)
                outs[branch][k1, 1, pl.ds(base, 32), :] = jnp.where(live, sine, 0.0)


def weight_kernel(scal, order, *refs):
    tiles, outs = refs[:-2], refs[-2:]
    freq = scal[0]
    rows, part = tiles[0].shape
    width = part * len(tiles)

    @pl.loop(0, rows // ROWS)
    def _(c):
        at = pl.ds(pl.multiple_of(c * ROWS, ROWS), ROWS)
        for j in range(width // 512):
            cols = slice(j * 512, (j + 1) * 512)
            first = j * 512 // part
            inside = slice(j * 512 - first * part, (j + 1) * 512 - first * part)
            here, there = tiles[first][at, inside], tiles[1 - first][at, inside]
            slowness = 1.0 / jnp.where(order[0] == 0, here, there)
            upper = jnp.clip((slowness - scal[1]) / (scal[2] - scal[1]), 0.0, 1.0)
            for branch, weight in enumerate((1.0 - upper, upper)):
                cosine, sine = circle(depth_step * freq * (slowness - scal[1 + branch]))
                outs[branch][0, at, cols] = weight * cosine
                outs[branch][1, at, cols] = weight * sine


def row_out(mat, work, out):
    outer, rows, double = work.shape
    inner = double // 2

    @pl.loop(0, outer // 2)
    def _(g):
        x = work[pl.ds(g * 2, 2)].reshape(2 * rows, double)
        y = product(halves(x), (mat[0], mat[1])).reshape(2, rows, double)
        for j in range(2):
            out[g * 2 + j, 0] = y[j, :, :inner]
            out[g * 2 + j, 1] = y[j, :, inner:]


def twiddled(real, imag, tw, k):
    c, s = tw[k, 0], tw[k, 1]
    return real * c - imag * s, real * s + imag * c


def conj_twiddled(real, imag, c, s):
    return real * c + imag * s, imag * c - real * s


def first_kernel(field, mat, tw, out, work):
    outer, rows, double = work.shape
    inner = double // 2

    @pl.loop(0, rows // ROWS)
    def _(c):
        at = pl.ds(pl.multiple_of(c * ROWS, ROWS), ROWS)
        real = [field[0, at, a * inner : (a + 1) * inner] for a in range(outer)]
        imag = [field[1, at, a * inner : (a + 1) * inner] for a in range(outer)]
        real, imag = small_fft(real, imag, -1)
        for k in range(outer):
            work[k, at, :inner], work[k, at, inner:] = twiddled(real[k], imag[k], tw, k)

    row_out(mat, work, out)


def column_forward_kernel(got, mat, tw, out, work):
    outer, _, rows, lanes = got.shape

    @pl.loop(0, rows // ROWS)
    def _(c):
        base = pl.multiple_of(c * ROWS, ROWS)
        at = pl.ds(base, ROWS)
        real = [got[a, 0, at, :] for a in range(outer)]
        imag = [got[a, 1, at, :] for a in range(outer)]
        real, imag = small_fft(real, imag, -1)
        for k in range(outer):
            cos, sin = tw[k, 0, at, :], tw[k, 1, at, :]
            work[k, 0, at, :] = real[k] * cos - imag[k] * sin
            work[k, 1, at, :] = real[k] * sin + imag[k] * cos

    @pl.loop(0, outer // 2)
    def _(g):
        x = [work[g * 2 + j].reshape(2 * rows, lanes) for j in range(2)]
        y = product((mat[0], mat[1]), halves(jnp.concatenate(x, axis=1)))
        for j in range(2):
            out[g * 2 + j] = y[:, j * lanes : (j + 1) * lanes].reshape(2, rows, lanes)


def column_back_kernel(spec, shift, mat, tw, out, work):
    outer, _, rows, lanes = spec.shape

    @pl.loop(0, outer // 2)
    def _(g):
        parts = []
        for j in range(2):
            k = g * 2 + j
            sr, si = spec[k, 0], spec[k, 1]
            er, ei = shift[k, 0], shift[k, 1]
            parts.append(jnp.concatenate([sr * er - si * ei, sr * ei + si * er], axis=0))
        y = product((mat[0], mat[1]), halves(jnp.concatenate(parts, axis=1)))
        for j in range(2):
            k = g * 2 + j
            z = y[:, j * lanes : (j + 1) * lanes]
            work[k, 0], work[k, 1] = conj_twiddled(z[:rows], z[rows:], tw[k, 0], tw[k, 1])

    @pl.loop(0, rows // ROWS)
    def _(c):
        at = pl.ds(pl.multiple_of(c * ROWS, ROWS), ROWS)
        real = [work[k, 0, at, :] for k in range(outer)]
        imag = [work[k, 1, at, :] for k in range(outer)]
        real, imag = small_fft(real, imag, 1)
        for a in range(outer):
            out[a, 0, at, :] = real[a]
            out[a, 1, at, :] = imag[a]


def row_back(got, mat, tw, work):
    outer, rows, double = work.shape
    inner = double // 2

    @pl.loop(0, outer // 2)
    def _(g):
        x = [jnp.concatenate([got[g * 2 + j, 0], got[g * 2 + j, 1]], axis=1) for j in range(2)]
        y = product(halves(jnp.concatenate(x, axis=0)), (mat[0], mat[1])).reshape(2, rows // ROWS, ROWS, double)
        for j in range(2):
            k = g * 2 + j
            c, s = tw[k, 0][None], tw[k, 1][None]
            real, imag = conj_twiddled(y[j, :, :, :inner], y[j, :, :, inner:], c, s)
            work[k, :, :inner] = real.reshape(rows, inner)
            work[k, :, inner:] = imag.reshape(rows, inner)


def row_back_kernel(got, weight, mat, tw, out, work):
    outer, rows, double = work.shape
    inner = double // 2
    row_back(got, mat, tw, work)

    @pl.loop(0, rows // ROWS)
    def _(c):
        at = pl.ds(pl.multiple_of(c * ROWS, ROWS), ROWS)
        real = [work[k, at, :inner] for k in range(outer)]
        imag = [work[k, at, inner:] for k in range(outer)]
        real, imag = small_fft(real, imag, 1)
        for a in range(outer):
            cols = slice(a * inner, (a + 1) * inner)
            wr, wi = weight[0, at, cols], weight[1, at, cols]
            out[0, at, cols] = real[a] * wr - imag[a] * wi
            out[1, at, cols] = real[a] * wi + imag[a] * wr


def row_join_kernel(last, got, weight, part, mat, tw, mat_next, out, work):
    outer, rows, double = work.shape
    inner = double // 2
    row_back(got, mat, tw, work)

    @pl.loop(0, rows // ROWS)
    def _(c):
        at = pl.ds(pl.multiple_of(c * ROWS, ROWS), ROWS)
        real = [work[k, at, :inner] for k in range(outer)]
        imag = [work[k, at, inner:] for k in range(outer)]
        real, imag = small_fft(real, imag, 1)
        new_real, new_imag = [], []
        for a in range(outer):
            cols = slice(a * inner, (a + 1) * inner)
            wr, wi = weight[0, at, cols], weight[1, at, cols]
            new_real.append(part[0, at, cols] + (real[a] * wr - imag[a] * wi))
            new_imag.append(part[1, at, cols] + (real[a] * wi + imag[a] * wr))
        if last:
            for a in range(outer):
                cols = slice(a * inner, (a + 1) * inner)
                out[0, at, cols] = new_real[a]
                out[1, at, cols] = new_imag[a]
        else:
            real, imag = small_fft(new_real, new_imag, -1)
            for k in range(outer):
                work[k, at, :inner], work[k, at, inner:] = twiddled(real[k], imag[k], tw, k)

    if not last:
        row_out(mat_next, work, out)


def call(body, shape, work, micros, *operands, scalars=0, outputs=1):
    in_specs = [pl.BlockSpec(memory_space=pltpu.SMEM)] * scalars
    in_specs += [pl.BlockSpec(memory_space=pltpu.VMEM)] * (len(operands) - scalars)
    result = jax.ShapeDtypeStruct(shape, jnp.float32)
    spec = pl.BlockSpec(memory_space=pltpu.VMEM)
    return pl.pallas_call(
        body,
        out_shape=result if outputs == 1 else (result,) * outputs,
        in_specs=in_specs,
        out_specs=spec if outputs == 1 else (spec,) * outputs,
        scratch_shapes=[pltpu.VMEM(work, jnp.float32)] if work else [],
        compiler_params=pltpu.CompilerParams(vmem_limit_bytes=VMEM_LIMIT),
        cost_estimate=pl.CostEstimate(flops=int(micros * 4e8), bytes_accessed=int(micros * 3e6), transcendentals=0),
    )(*operands)


def shards(wavefield, freqs, velocity, ref_slow):
    slabs = lax.axis_size("slab")
    slab_index = lax.axis_index("slab")
    rows = wavefield.shape[2]
    width_x = rows * slabs
    width_y = wavefield.shape[3]
    columns = width_y // slabs
    depth = ref_slow.shape[0]
    across = (slabs, 2, rows, columns)
    row_fwd = matrix_of(columns, width_y, -1, False)
    row_inv = matrix_of(columns, width_y, 1, False)
    col_fwd = matrix_of(rows, width_x, -1, True)
    col_inv = matrix_of(rows, width_x, 1, True)
    row_tw = twiddle_table(slabs, columns, False)
    col_tw = twiddle_table(slabs, rows, True)
    row_work = (slabs, rows, 2 * columns)

    freq_count = lax.axis_size("freq")
    group = slabs // freq_count
    run = group // freq_count
    row = lax.axis_index("freq")
    both = ("freq", "slab")
    everyone = [(y, s) for y in range(freq_count) for s in range(slabs)]

    def owner(slab):
        return (slab // run) % freq_count, (slab // group) * run + slab % run

    def device(y, g, place):
        return y * slabs + g * group + place

    members = []
    for g in range(freq_count):
        members.append([device(y, g, place) for y, place in map(owner, range(slabs))])
    here = lax.rem(slab_index, group)
    mine = (here // run) * group + row * run + lax.rem(here, run)

    def swap(x, name):
        return lax.all_to_all(x, name, split_axis=0, concat_axis=0, tiled=True)

    def exchange(x):
        return lax.all_to_all(x, both, split_axis=0, concat_axis=0, tiled=True, axis_index_groups=members)

    home = [(y * slabs + s, (s // group) * slabs + y * group + s % group) for y, s in everyone]
    group_freq = lax.ppermute(freqs, both, home)

    number = mine + slabs * jnp.arange(columns, dtype=jnp.int32)
    number = jnp.where(number < width_y // 2, number, number - width_y)
    along_y = number.astype(jnp.float32) / width_y
    fy2 = jnp.broadcast_to((along_y * along_y)[None, :], (ROWS, columns))

    part_send = call(first_kernel, across, row_work, 4, wavefield[:, 0], row_fwd, row_tw)
    sends = part_send.reshape(freq_count, freq_count, run, 2, rows, columns)
    sends = sends.swapaxes(0, 1).reshape(across)
    got = swap(swap(sends, "freq"), "slab")

    def grouped_velocity(values):
        moved = []
        for shift in range(freq_count):
            route = []
            for y, s in everyone:
                to_row, place = owner(s)
                route.append((y * slabs + s, device(to_row, (to_row + y + shift) % freq_count, place)))
            moved.append(lax.ppermute(values, both, route))
        return moved

    order = ((slab_index // group + freq_count - row) % freq_count).astype(jnp.int32)[None]

    for level in range(depth):
        last = level == depth - 1
        if level:
            got = exchange(part_send)
        else:
            got, velocity = lax.optimization_barrier((got, velocity))
        tiles = grouped_velocity(velocity[level])
        scal = jnp.concatenate([group_freq, ref_slow[level]])
        shift = call(
            functools.partial(spread_kernel, slabs, width_x), across, None, 8, scal, fy2, scalars=1, outputs=2
        )
        weight = call(weight_kernel, (2, rows, width_y), None, 8, scal, order, *tiles, scalars=2, outputs=2)
        spec = call(column_forward_kernel, across, across, 7, got, col_fwd, col_tw)
        back = []
        for branch in range(2):
            sent = call(column_back_kernel, across, across, 7, spec, shift[branch], col_inv, col_tw)
            back.append(exchange(sent))
        part = call(row_back_kernel, (2, rows, width_y), row_work, 6, back[0], weight[0], row_inv, row_tw)
        part_send = call(
            functools.partial(row_join_kernel, last),
            (2, rows, width_y) if last else across,
            row_work, 9, back[1], weight[1], part, row_inv, row_tw, row_fwd,
        )
    leave = []
    for y, s in everyone:
        to_row, place = owner(s)
        leave.append((device(to_row, y, place), y * slabs + s))
    return lax.ppermute(part_send, both, leave)[:, None]


def solution(mesh):
    slabs = mesh.shape["slab"]

    def program(wavefield, freqs, velocity, ref_slow):
        width_x, width_y = wavefield.shape[2:]
        whole_tiles = (
            width_y // slabs == LANES
            and width_x // slabs == LANES
            and wavefield.shape[1] == mesh.shape["freq"] == 2
            and slabs % 4 == 0
        )
        step = jax.shard_map(
            shards if whole_tiles else shards_generic,
            mesh=mesh,
            in_specs=(P(None, "freq", "slab", None), P("freq"), P(None, "slab", "freq"), P()),
            out_specs=P(None, "freq", "slab", None),
            check_vma=False,
        )
        return step(wavefield, freqs, velocity, ref_slow)

    return program
```

```python
import functools
import math

import jax
import jax.numpy as jnp
import numpy as np
from jax import lax
from jax.experimental import pallas as pl
from jax.experimental.pallas import tpu as pltpu
from jax.sharding import PartitionSpec as P

two_pi = 2.0 * math.pi
depth_step = 2.0


def dft_matrix(length, sign):
    index = jnp.arange(length, dtype=jnp.int32)
    product = index[:, None] * index[None, :] % length
    angle = sign * two_pi / length * product.astype(jnp.float32)
    scale = 1.0 / math.sqrt(length)
    return (jnp.cos(angle) * scale, jnp.sin(angle) * scale)


def twiddle(outer, inner, sign):
    length = outer * inner
    product = (
        jnp.arange(outer, dtype=jnp.int32)[:, None]
        * jnp.arange(inner, dtype=jnp.int32)[None, :]
        % length
    )
    angle = sign * two_pi / length * product.astype(jnp.float32)
    return (jnp.cos(angle), jnp.sin(angle))


def complex_mix(form, mat_real, mat_imag, data_real, data_imag):

    def product(matrix, data):
        return jnp.einsum(form, matrix, data, precision=lax.Precision.HIGHEST)

    return (
        product(mat_real, data_real) - product(mat_imag, data_imag),
        product(mat_real, data_imag) + product(mat_imag, data_real),
    )


def transform(real, imag, trailing, sign):
    length = real.shape[-2] if trailing else real.shape[-1]
    inner = min(length, 128)
    outer = length // inner
    outer_real, outer_imag = dft_matrix(outer, sign)
    inner_real, inner_imag = dft_matrix(inner, sign)
    turn_real, turn_imag = twiddle(outer, inner, sign)
    if trailing:
        leading = real.shape[:-2]
        tail = real.shape[-1:]
        form_outer = "ka,...abm->...kbm"
        form_inner = "bj,...kbm->...kjm"
        turn_real = turn_real[:, :, None]
        turn_imag = turn_imag[:, :, None]
    else:
        leading = real.shape[:-1]
        tail = ()
        form_outer = "ka,...ab->...kb"
        form_inner = "bj,...kb->...kj"
    split_shape = leading + (outer, inner) + tail
    real = real.reshape(split_shape)
    imag = imag.reshape(split_shape)
    if sign < 0:
        real, imag = complex_mix(form_outer, outer_real, outer_imag, real, imag)
        real, imag = (real * turn_real - imag * turn_imag, real * turn_imag + imag * turn_real)
        real, imag = complex_mix(form_inner, inner_real, inner_imag, real, imag)
    else:
        real, imag = complex_mix(form_inner, inner_real, inner_imag, real, imag)
        real, imag = (real * turn_real - imag * turn_imag, real * turn_imag + imag * turn_real)
        real, imag = complex_mix(form_outer, outer_real, outer_imag, real, imag)
    joined = leading + (length,) + tail
    return (real.reshape(joined), imag.reshape(joined))


def wave_numbers(positions, length):
    inner = min(length, 128)
    outer = length // inner
    number = positions // inner + outer * (positions % inner)
    number = jnp.where(number < length // 2, number, number - length)
    return number.astype(jnp.float32) / length


def forward_x(items):
    real, imag = transform(items[0], items[1], True, -1)
    return jnp.stack((real, imag))


def inverse_y(items):
    real, imag = transform(items[:, 0], items[:, 1], False, 1)
    return jnp.stack((real, imag), axis=1)


def shards_generic(wavefield, freqs, velocity, ref_slow):
    slabs = lax.axis_size("slab")
    slab_index = lax.axis_index("slab")
    rows = wavefield.shape[2]
    width_x = rows * slabs
    width_y = wavefield.shape[3]
    columns = width_y // slabs
    depth = ref_slow.shape[0]
    along_x = wave_numbers(jnp.arange(width_x, dtype=jnp.int32), width_x)
    along_y = wave_numbers(slab_index * columns + jnp.arange(columns, dtype=jnp.int32), width_y)
    square = along_x[:, None] ** 2 + along_y[None, :] ** 2
    freq_col = freqs[:, None, None]

    def advance(level, field):
        local_tile = lax.dynamic_index_in_dim(velocity, level, 0, keepdims=False)
        tile = lax.all_gather(local_tile, "freq", axis=1, tiled=True)
        real, imag = transform(field[0], field[1], False, -1)
        spectrum = forward_x(
            lax.all_to_all(jnp.stack((real, imag)), "slab", split_axis=3, concat_axis=2, tiled=True)
        )
        slow_pair = lax.dynamic_index_in_dim(ref_slow, level, 0, keepdims=False)
        slowness = 1.0 / tile
        upper_weight = jnp.clip((slowness - slow_pair[0]) / (slow_pair[1] - slow_pair[0]), 0.0, 1.0)
        weights = [1.0 - upper_weight, upper_weight]
        shifted = []
        for branch in range(2):
            target = (freq_col * slow_pair[branch]) ** 2 - square[None]
            angle = two_pi * depth_step * jnp.sqrt(jnp.abs(target))
            live = target >= 0
            prop_real = jnp.where(live, jnp.cos(angle), jnp.exp(-angle))
            prop_imag = jnp.where(live, jnp.sin(angle), jnp.zeros_like(angle))
            spec_real = spectrum[0] * prop_real - spectrum[1] * prop_imag
            spec_imag = spectrum[0] * prop_imag + spectrum[1] * prop_real
            back_real, back_imag = transform(spec_real, spec_imag, True, 1)
            shifted.append(jnp.stack((back_real, back_imag)))
        pieces = []
        for branch in range(2):
            moved = lax.all_to_all(shifted[branch], "slab", split_axis=2, concat_axis=3, tiled=True)
            pieces.append(inverse_y(moved[None])[0])
        spatial = jnp.stack(pieces)
        new_real = jnp.zeros_like(field[0])
        new_imag = jnp.zeros_like(field[1])
        for branch in range(2):
            theta = two_pi * depth_step * freq_col * (slowness - slow_pair[branch])[None]
            weight = weights[branch][None]
            cosine = jnp.cos(theta)
            sine = jnp.sin(theta)
            part_real = spatial[branch, 0]
            part_imag = spatial[branch, 1]
            new_real = new_real + weight * (cosine * part_real - sine * part_imag)
            new_imag = new_imag + weight * (cosine * part_imag + sine * part_real)
        return jnp.stack((new_real, new_imag))

    return lax.fori_loop(0, depth, advance, wavefield)


LANES = 128
ROWS = 8
VMEM_LIMIT = 56 * 2**20


def turn(numerator, denominator, sign):
    angle = sign * 2.0 * np.pi * ((numerator % denominator) / denominator)
    return (np.cos(angle), np.sin(angle))


def times(real, imag, c, s):
    if abs(s) < 1e-12:
        return (real, imag) if c > 0 else (-real, -imag)
    if abs(c) < 1e-12:
        return (-imag, real) if s > 0 else (imag, -real)
    if abs(abs(c) - abs(s)) < 1e-12:
        k = float(abs(c))
        a, b = (k if c > 0 else -k), (s > 0) == (c > 0)
        if b:
            return ((real - imag) * a, (real + imag) * a)
        return ((real + imag) * a, (imag - real) * a)
    c, s = float(c), float(s)
    return (real * c - imag * s, real * s + imag * c)


def small_fft(real, imag, sign):
    count = len(real)
    if count == 1:
        return real, imag
    er, ei = small_fft(real[0::2], imag[0::2], sign)
    odd_r, odd_i = small_fft(real[1::2], imag[1::2], sign)
    low, high = [], []
    for k in range(count // 2):
        tr, ti = times(odd_r[k], odd_i[k], *turn(k, count, sign))
        low.append((er[k] + tr, ei[k] + ti))
        high.append((er[k] - tr, ei[k] - ti))
    both = low + high
    return [v[0] for v in both], [v[1] for v in both]


def halves(x):
    high = x.astype(jnp.bfloat16)
    low = (x - high.astype(jnp.float32)).astype(jnp.bfloat16)
    return high, low


def product(a, b):
    def dot(p, q):
        return jnp.dot(p, q, preferred_element_type=jnp.float32)

    return dot(a[0], b[0]) + (dot(a[0], b[1]) + dot(a[1], b[0]))


def matrix_of(inner, length, sign, left):
    index = np.arange(inner)
    angle = sign * 2.0 * np.pi * ((index[:, None] * index[None, :]) % inner) / inner
    c = np.cos(angle) / np.sqrt(length)
    s = np.sin(angle) / np.sqrt(length)
    full = np.block([[c, -s], [s, c]]) if left else np.block([[c, s], [-s, c]])
    full = full.astype(np.float32)
    high = full.astype(jnp.bfloat16)
    low = (full - high.astype(np.float32)).astype(jnp.bfloat16)
    return np.stack([high, low])


def twiddle_table(outer, inner, rows):
    c, s = turn(np.arange(outer)[:, None] * np.arange(inner)[None, :], outer * inner, -1)
    both = np.stack([c, s], axis=1).astype(np.float32)
    if rows:
        return np.ascontiguousarray(np.broadcast_to(both[:, :, :, None], (outer, 2, inner, LANES)))
    return np.ascontiguousarray(np.broadcast_to(both[:, :, None, :], (outer, 2, ROWS, inner)))


def cosine_terms():
    z = 0.125 + 0.125 * np.cos(np.pi * (np.arange(400) + 0.5) / 400)
    r = np.sqrt(z)

    def fit(values, degree):
        poly = np.polynomial.Chebyshev.fit(z, values, degree, domain=[0.0, 0.25])
        poly = poly.convert(kind=np.polynomial.Polynomial)
        return [float(np.float32(v)) for v in poly.coef]

    return fit(np.cos(2 * np.pi * r), 8), fit(np.sin(2 * np.pi * r) / r, 7)


COS_TERMS, SIN_TERMS = cosine_terms()


def horner(terms, z):
    value = z * terms[-1] + terms[-2]
    for term in terms[-3::-1]:
        value = value * z + term
    return value


def circle(turns):
    rest = turns - jnp.round(turns)
    z = rest * rest
    return horner(COS_TERMS, z), rest * horner(SIN_TERMS, z)


def spread_kernel(outer, length, scal, fy2, *outs):
    freq = scal[0]
    rows = outs[0].shape[2]

    @pl.loop(0, outer)
    def _(k1):
        @pl.loop(0, rows // 32)
        def _(c):
            base = pl.multiple_of(c * 32, 32)
            number = k1 + outer * (base + lax.broadcasted_iota(jnp.int32, (32, LANES), 0))
            number = jnp.where(number < length // 2, number, number - length)
            fx = number.astype(jnp.float32) * (1.0 / length)
            square = fx * fx + fy2[0:1, :]
            for branch in range(2):
                wave = freq * scal[1 + branch]
                target = wave * wave - square
                turns = depth_step * jnp.sqrt(jnp.abs(target))
                live = target >= 0
                cosine, sine = circle(turns)
                decay = jnp.exp(turns * (-two_pi))
                outs[branch][k1, 0, pl.ds(base, 32), :] = jnp.where(live, cosine, decay)
                outs[branch][k1, 1, pl.ds(base, 32), :] = jnp.where(live, sine, 0.0)


def weight_kernel(scal, order, *refs):
    tiles, outs = refs[:-2], refs[-2:]
    freq = scal[0]
    rows, part = tiles[0].shape
    width = part * len(tiles)

    @pl.loop(0, rows // ROWS)
    def _(c):
        at = pl.ds(pl.multiple_of(c * ROWS, ROWS), ROWS)
        for j in range(width // 512):
            cols = slice(j * 512, (j + 1) * 512)
            first = j * 512 // part
            inside = slice(j * 512 - first * part, (j + 1) * 512 - first * part)
            here, there = tiles[first][at, inside], tiles[1 - first][at, inside]
            slowness = 1.0 / jnp.where(order[0] == 0, here, there)
            upper = jnp.clip((slowness - scal[1]) / (scal[2] - scal[1]), 0.0, 1.0)
            for branch, weight in enumerate((1.0 - upper, upper)):
                cosine, sine = circle(depth_step * freq * (slowness - scal[1 + branch]))
                outs[branch][0, at, cols] = weight * cosine
                outs[branch][1, at, cols] = weight * sine


def row_out(mat, work, out, spot=lambda k: k):
    outer, rows, double = work.shape
    inner = double // 2

    @pl.loop(0, outer // 2)
    def _(g):
        x = work[pl.ds(g * 2, 2)].reshape(2 * rows, double)
        y = product(halves(x), (mat[0], mat[1])).reshape(2, rows, double)
        for j in range(2):
            out[spot(g * 2 + j), 0] = y[j, :, :inner]
            out[spot(g * 2 + j), 1] = y[j, :, inner:]


def twiddled(real, imag, tw, k):
    c, s = tw[k, 0], tw[k, 1]
    return real * c - imag * s, real * s + imag * c


def conj_twiddled(real, imag, c, s):
    return real * c + imag * s, imag * c - real * s


def first_kernel(start, spot, field, mat, tw, out, work):
    outer, rows, double = work.shape
    inner = double // 2

    @pl.loop(0, rows // ROWS)
    def _(c):
        base = pl.multiple_of(c * ROWS, ROWS)
        at, source = pl.ds(base, ROWS), pl.ds(start + base, ROWS)
        real = [field[0, source, a * inner : (a + 1) * inner] for a in range(outer)]
        imag = [field[1, source, a * inner : (a + 1) * inner] for a in range(outer)]
        real, imag = small_fft(real, imag, -1)
        for k in range(outer):
            work[k, at, :inner], work[k, at, inner:] = twiddled(real[k], imag[k], tw, k)

    row_out(mat, work, out, spot)


def column_forward_kernel(*refs):
    pieces, (mat, tw, out, work) = refs[:-4], refs[-4:]
    outer, _, rows, lanes = out.shape
    part = rows // len(pieces)

    for index, got in enumerate(pieces):

        @pl.loop(0, part // ROWS)
        def _(c):
            base = pl.multiple_of(c * ROWS, ROWS)
            source, at = pl.ds(base, ROWS), pl.ds(index * part + base, ROWS)
            real = [got[a, 0, source, :] for a in range(outer)]
            imag = [got[a, 1, source, :] for a in range(outer)]
            real, imag = small_fft(real, imag, -1)
            for k in range(outer):
                cos, sin = tw[k, 0, at, :], tw[k, 1, at, :]
                work[k, 0, at, :] = real[k] * cos - imag[k] * sin
                work[k, 1, at, :] = real[k] * sin + imag[k] * cos

    @pl.loop(0, outer // 2)
    def _(g):
        x = [work[g * 2 + j].reshape(2 * rows, lanes) for j in range(2)]
        y = product((mat[0], mat[1]), halves(jnp.concatenate(x, axis=1)))
        for j in range(2):
            out[g * 2 + j] = y[:, j * lanes : (j + 1) * lanes].reshape(2, rows, lanes)


def column_back_kernel(spec, shift, mat, tw, out, work):
    outer, _, rows, lanes = spec.shape

    @pl.loop(0, outer // 2)
    def _(g):
        parts = []
        for j in range(2):
            k = g * 2 + j
            sr, si = spec[k, 0], spec[k, 1]
            er, ei = shift[k, 0], shift[k, 1]
            parts.append(jnp.concatenate([sr * er - si * ei, sr * ei + si * er], axis=0))
        y = product((mat[0], mat[1]), halves(jnp.concatenate(parts, axis=1)))
        for j in range(2):
            k = g * 2 + j
            z = y[:, j * lanes : (j + 1) * lanes]
            work[k, 0], work[k, 1] = conj_twiddled(z[:rows], z[rows:], tw[k, 0], tw[k, 1])

    @pl.loop(0, rows // ROWS)
    def _(c):
        at = pl.ds(pl.multiple_of(c * ROWS, ROWS), ROWS)
        real = [work[k, 0, at, :] for k in range(outer)]
        imag = [work[k, 1, at, :] for k in range(outer)]
        real, imag = small_fft(real, imag, 1)
        for a in range(outer):
            out[a, 0, at, :] = real[a]
            out[a, 1, at, :] = imag[a]


def row_back(got, mat, tw, work):
    outer, rows, double = work.shape
    inner = double // 2

    @pl.loop(0, outer // 2)
    def _(g):
        x = [jnp.concatenate([got[g * 2 + j, 0], got[g * 2 + j, 1]], axis=1) for j in range(2)]
        y = product(halves(jnp.concatenate(x, axis=0)), (mat[0], mat[1])).reshape(2, rows // ROWS, ROWS, double)
        for j in range(2):
            k = g * 2 + j
            c, s = tw[k, 0][None], tw[k, 1][None]
            real, imag = conj_twiddled(y[j, :, :, :inner], y[j, :, :, inner:], c, s)
            work[k, :, :inner] = real.reshape(rows, inner)
            work[k, :, inner:] = imag.reshape(rows, inner)


def row_back_kernel(got, weight, mat, tw, out, work):
    outer, rows, double = work.shape
    inner = double // 2
    row_back(got, mat, tw, work)

    @pl.loop(0, rows // ROWS)
    def _(c):
        at = pl.ds(pl.multiple_of(c * ROWS, ROWS), ROWS)
        real = [work[k, at, :inner] for k in range(outer)]
        imag = [work[k, at, inner:] for k in range(outer)]
        real, imag = small_fft(real, imag, 1)
        for a in range(outer):
            cols = slice(a * inner, (a + 1) * inner)
            wr, wi = weight[0, at, cols], weight[1, at, cols]
            out[0, at, cols] = real[a] * wr - imag[a] * wi
            out[1, at, cols] = real[a] * wi + imag[a] * wr


def row_join_kernel(last, got, weight, part, mat, tw, mat_next, out, work):
    outer, rows, double = work.shape
    inner = double // 2
    row_back(got, mat, tw, work)

    @pl.loop(0, rows // ROWS)
    def _(c):
        at = pl.ds(pl.multiple_of(c * ROWS, ROWS), ROWS)
        real = [work[k, at, :inner] for k in range(outer)]
        imag = [work[k, at, inner:] for k in range(outer)]
        real, imag = small_fft(real, imag, 1)
        new_real, new_imag = [], []
        for a in range(outer):
            cols = slice(a * inner, (a + 1) * inner)
            wr, wi = weight[0, at, cols], weight[1, at, cols]
            new_real.append(part[0, at, cols] + (real[a] * wr - imag[a] * wi))
            new_imag.append(part[1, at, cols] + (real[a] * wi + imag[a] * wr))
        if last:
            for a in range(outer):
                cols = slice(a * inner, (a + 1) * inner)
                out[0, at, cols] = new_real[a]
                out[1, at, cols] = new_imag[a]
        else:
            real, imag = small_fft(new_real, new_imag, -1)
            for k in range(outer):
                work[k, at, :inner], work[k, at, inner:] = twiddled(real[k], imag[k], tw, k)

    if not last:
        row_out(mat_next, work, out)


def call(body, shape, work, micros, *operands, scalars=0, outputs=1):
    in_specs = [pl.BlockSpec(memory_space=pltpu.SMEM)] * scalars
    in_specs += [pl.BlockSpec(memory_space=pltpu.VMEM)] * (len(operands) - scalars)
    result = jax.ShapeDtypeStruct(shape, jnp.float32)
    spec = pl.BlockSpec(memory_space=pltpu.VMEM)
    return pl.pallas_call(
        body,
        out_shape=result if outputs == 1 else (result,) * outputs,
        in_specs=in_specs,
        out_specs=spec if outputs == 1 else (spec,) * outputs,
        scratch_shapes=[pltpu.VMEM(work, jnp.float32)] if work else [],
        compiler_params=pltpu.CompilerParams(vmem_limit_bytes=VMEM_LIMIT),
        cost_estimate=pl.CostEstimate(flops=int(micros * 4e8), bytes_accessed=int(micros * 3e6), transcendentals=0),
    )(*operands)


def shards(wavefield, freqs, velocity, ref_slow):
    slabs = lax.axis_size("slab")
    slab_index = lax.axis_index("slab")
    rows = wavefield.shape[2]
    width_x = rows * slabs
    width_y = wavefield.shape[3]
    columns = width_y // slabs
    depth = ref_slow.shape[0]
    across = (slabs, 2, rows, columns)
    row_fwd = matrix_of(columns, width_y, -1, False)
    row_inv = matrix_of(columns, width_y, 1, False)
    col_fwd = matrix_of(rows, width_x, -1, True)
    col_inv = matrix_of(rows, width_x, 1, True)
    row_tw = twiddle_table(slabs, columns, False)
    col_tw = twiddle_table(slabs, rows, True)
    row_work = (slabs, rows, 2 * columns)

    freq_count = lax.axis_size("freq")
    group = slabs // freq_count
    run = group // freq_count
    row = lax.axis_index("freq")
    both = ("freq", "slab")
    everyone = [(y, s) for y in range(freq_count) for s in range(slabs)]

    def owner(slab):
        return (slab // run) % freq_count, (slab // group) * run + slab % run

    def device(y, g, place):
        return y * slabs + g * group + place

    members = []
    for g in range(freq_count):
        members.append([device(y, g, place) for y, place in map(owner, range(slabs))])
    here = lax.rem(slab_index, group)
    mine = (here // run) * group + row * run + lax.rem(here, run)

    def swap(x, name):
        return lax.all_to_all(x, name, split_axis=0, concat_axis=0, tiled=True)

    def exchange(x):
        return lax.all_to_all(x, both, split_axis=0, concat_axis=0, tiled=True, axis_index_groups=members)

    home = [(y * slabs + s, (s // group) * slabs + y * group + s % group) for y, s in everyone]
    group_freq = lax.ppermute(freqs, both, home)

    number = mine + slabs * jnp.arange(columns, dtype=jnp.int32)
    number = jnp.where(number < width_y // 2, number, number - width_y)
    along_y = number.astype(jnp.float32) / width_y
    fy2 = jnp.broadcast_to((along_y * along_y)[None, :], (ROWS, columns))

    def spot(k):
        return (k // run) % freq_count * group + k // group * run + k % run

    half = rows // 2
    got = []
    for piece in range(2):
        sends = call(
            functools.partial(first_kernel, piece * half, spot), (slabs, 2, half, columns),
            (slabs, half, 2 * columns), 3, wavefield[:, 0], row_fwd, row_tw,
        )
        keep = lax.dynamic_slice_in_dim(sends, row * group, group, 0)
        give = lax.dynamic_slice_in_dim(sends, (1 - row) * group, group, 0)
        came = lax.ppermute(give, "freq", [(0, 1), (1, 0)])
        pair = [jnp.where(row == y, keep, came) for y in range(freq_count)]
        sends = jnp.concatenate(pair, axis=0)
        got.append(swap(sends, "slab"))

    def grouped_velocity(values):
        moved = []
        for shift in range(freq_count):
            route = []
            for y, s in everyone:
                to_row, place = owner(s)
                route.append((y * slabs + s, device(to_row, (to_row + y + shift) % freq_count, place)))
            moved.append(lax.ppermute(values, both, route))
        return moved

    order = ((slab_index // group + freq_count - row) % freq_count).astype(jnp.int32)[None]

    for level in range(depth):
        last = level == depth - 1
        if level:
            got = [exchange(part_send)]
        else:
            got, velocity = lax.optimization_barrier((got, velocity))
        tiles = grouped_velocity(velocity[level])
        scal = jnp.concatenate([group_freq, ref_slow[level]])
        shift = call(
            functools.partial(spread_kernel, slabs, width_x), across, None, 8, scal, fy2, scalars=1, outputs=2
        )
        weight = call(weight_kernel, (2, rows, width_y), None, 8, scal, order, *tiles, scalars=2, outputs=2)
        spec = call(column_forward_kernel, across, across, 7, *got, col_fwd, col_tw)
        back = []
        for branch in range(2):
            sent = call(column_back_kernel, across, across, 7, spec, shift[branch], col_inv, col_tw)
            back.append(exchange(sent))
        part = call(row_back_kernel, (2, rows, width_y), row_work, 6, back[0], weight[0], row_inv, row_tw)
        part_send = call(
            functools.partial(row_join_kernel, last),
            (2, rows, width_y) if last else across,
            row_work, 9, back[1], weight[1], part, row_inv, row_tw, row_fwd,
        )
    leave = []
    for y, s in everyone:
        to_row, place = owner(s)
        leave.append((device(to_row, y, place), y * slabs + s))
    return lax.ppermute(part_send, both, leave)[:, None]


def solution(mesh):
    slabs = mesh.shape["slab"]

    def program(wavefield, freqs, velocity, ref_slow):
        width_x, width_y = wavefield.shape[2:]
        whole_tiles = (
            width_y // slabs == LANES
            and width_x // slabs == LANES
            and wavefield.shape[1] == mesh.shape["freq"] == 2
            and slabs % 4 == 0
        )
        step = jax.shard_map(
            shards if whole_tiles else shards_generic,
            mesh=mesh,
            in_specs=(P(None, "freq", "slab", None), P("freq"), P(None, "slab", "freq"), P()),
            out_specs=P(None, "freq", "slab", None),
            check_vma=False,
        )
        return step(wavefield, freqs, velocity, ref_slow)

    return program
```
